256 devices in a mesh: tiles: 16 (over y, z_lo, core), coef: 16 (over x, z_hi).
Axes of the slice: x: 4, y: 4, z: 8 (z_hi: 4, z_lo: 2; z = z_hi * 2 + z_lo), core: 2. Of those that a mesh axis runs over, the one named last changes fastest.
Arguments:
- fields: bfloat16 [256, 8192], P('coef', 'tiles'), may hold values from -6 to 6
- adjoints: bfloat16 [256, 8192], P('coef', 'tiles'), may hold values from -6 to 6
- couple: bfloat16 [30, 256, 256], replicated, may hold values from -0.0625 to 0.0625
- tmatrices: bfloat16 [64, 256, 256], P('tiles', 'coef'), may hold values from -0.375 to 0.375
- neighbours: int32 [8192, 30], P('tiles'), may hold values from -1 to 8191, as said below
- classes: int32 [8192], P('tiles'), may hold values from 0 to 63
Outputs:
- forward_out: bfloat16 [256, 8192], P('coef', 'tiles')
- adjoint_out: bfloat16 [256, 8192], P('coef', 'tiles')
The draws below stay inside these ranges and needn't reach their ends.
Inputs may be any that keep to these rules, and one draw needn't show every extreme that they name: neighbours[i, m] is -1 or i + m - 15 for m < 15, or i + m - 14 for m >= 15; links are mutual: neighbours[i, m] = j >= 0 exactly when neighbours[j, 29 - m] = i; slots 15 - 1 and 15 are filled wherever the neighbouring pillar exists.
All inputs are finite; a program needn't handle non-finite values.
Results may differ from the reference program's by a relative error of at most 0.0037.
Values may be sent and summed in bfloat16 or wider, within the bound.
A program may use at most 64 MiB of HBM per device.

```python
import jax
import jax.numpy as jnp
from jax import lax

KR = 256
SLOTS = 30
HW = 15
PILLARS = 8192
CLASSES = 64


def draw_neighbours(key, part):
    link_bits = jax.random.randint(key, (PILLARS, HW), 0, 5)
    keep_link = link_bits < 4
    keep_link = keep_link.at[:, 0].set(True)
    slot_ids = jnp.arange(SLOTS, dtype=jnp.int32)
    offsets = jnp.where(slot_ids < HW, slot_ids - HW, slot_ids - HW + 1)
    pillar_ids = jnp.arange(PILLARS, dtype=jnp.int32)[:, None]
    targets = pillar_ids + offsets[None, :]
    lower = jnp.clip(jnp.minimum(pillar_ids, targets), 0, PILLARS - 1)
    distance = jnp.abs(offsets)[None, :] - 1
    inside = (targets >= 0) & (targets < PILLARS)
    kept = keep_link[lower, distance]
    return jnp.where(inside & kept, targets, -1).astype(jnp.int32)


def set_ends(drawn, own_key, least, top_value):
    longest = drawn.shape.index(max(drawn.shape))
    spots = []
    for shift in (0, 1):
        where = [jax.random.randint(jax.random.fold_in(own_key, axis), (), 0, length) for axis, length in enumerate(drawn.shape)]
        where[longest] = (where[longest] + shift) % drawn.shape[longest]
        spots.append(tuple(where))
    return drawn.at[spots[0]].set(least).at[spots[1]].set(top_value)


def levels(own_key, dims, split, smallest, largest):
    factor_of, own = 1.0, jax.random.fold_in(own_key, 6)
    for axis_at, blocks in split:
        heights = jnp.exp(jax.random.uniform(jax.random.fold_in(own, axis_at), (blocks,), jnp.float32, smallest / len(split), largest / len(split)))
        factor_of = factor_of * jnp.repeat(heights, dims[axis_at] // blocks).reshape([-1 if axis == axis_at else 1 for axis in range(len(dims))])
    return factor_of


def normal_values(rng, shape, deviation, bound, split=(), held_as=jnp.bfloat16):
    array = deviation * jax.random.normal(rng, shape, jnp.float32)
    if split:
        array = array * levels(rng, shape, split, -0.22, 0.18)
    return jnp.clip(array, -bound, bound).astype(held_as)


def setup_inputs(seed: int = 0) -> dict:
    splits = jax.random.split(jax.random.key(seed), 7)
    return {
        "fields": normal_values(splits[0], (KR, PILLARS), 1.0, 6.0, ((0, 16), (1, 16))),
        "adjoints": normal_values(splits[1], (KR, PILLARS), 1.0, 6.0, ((0, 16), (1, 16))),
        "couple": normal_values(splits[2], (SLOTS, KR, KR), (SLOTS * KR) ** -0.5, 0.0625),
        "tmatrices": normal_values(splits[3], (CLASSES, KR, KR), KR ** -0.5, 0.375, ((0, 16), (1, 16))),
        "neighbours": draw_neighbours(jax.random.fold_in(splits[6], 71), 0),
        "classes": set_ends(jax.random.randint(splits[5], (PILLARS,), 0, CLASSES), jax.random.fold_in(splits[5], 1), 0, CLASSES - 1).astype(jnp.int32),
    }


def pair_sum(source, couple, slot_index, slot_weight, adjoint_mode):
    def accumulate(running, slot_id):
        selected = jnp.take(source, slot_index[:, slot_id], axis=1) * slot_weight[:, slot_id][None, :]
        if adjoint_mode:
            matrix = lax.dynamic_index_in_dim(couple, SLOTS - 1 - slot_id, 0, keepdims=False).T
        else:
            matrix = lax.dynamic_index_in_dim(couple, slot_id, 0, keepdims=False)
        return running + jnp.dot(matrix, selected, preferred_element_type=jnp.float32), None

    start_sum = jnp.zeros((KR, PILLARS), jnp.float32)
    result, unused = lax.scan(accumulate, start_sum, jnp.arange(SLOTS, dtype=jnp.int32))
    return result


def class_apply(vectors, tmatrices, classes, adjoint_mode):
    block_len = 32
    count_blocks = PILLARS // block_len
    shaped = vectors.astype(jnp.float32).reshape(KR, count_blocks, block_len).transpose(1, 0, 2)
    grouped = classes.reshape(count_blocks, block_len)

    def one_block(inputs):
        labels, values = inputs
        matrices = jnp.take(tmatrices, labels, axis=0).astype(jnp.float32)
        if adjoint_mode:
            return jnp.einsum("irk,ri->ki", matrices, values)
        return jnp.einsum("irk,ki->ri", matrices, values)

    output = lax.map(one_block, (grouped, shaped))
    return output.transpose(1, 0, 2).reshape(KR, PILLARS)


def reference(fields, adjoints, couple, tmatrices, neighbours, classes):
    is_valid = neighbours >= 0
    slot_index = jnp.where(is_valid, neighbours, 0).astype(jnp.int32)
    slot_weight = is_valid.astype(fields.dtype)
    coupled = pair_sum(fields, couple, slot_index, slot_weight, False).astype(jnp.bfloat16)
    forward_out = (fields.astype(jnp.float32) - class_apply(coupled, tmatrices, classes, False)).astype(jnp.bfloat16)
    scattered = class_apply(adjoints, tmatrices, classes, True).astype(jnp.bfloat16)
    adjoint_out = (adjoints.astype(jnp.float32) - pair_sum(scattered, couple, slot_index, slot_weight, True)).astype(jnp.bfloat16)
    return forward_out, adjoint_out
```

```python
import functools

import jax
import jax.numpy as jnp
from jax import lax
from jax.experimental import pallas as pl
from jax.experimental.pallas import tpu as pltpu
from jax.sharding import PartitionSpec as P

SLOTS = 30
HW = 15
LANE = 128
MESH = pl.DeviceIdType.MESH
F32 = jnp.float32
BF16 = jnp.bfloat16


def dims(lhs, rhs):
    return (((lhs,), (rhs,)), ((), ()))


def dot(a, b, lhs=1, rhs=0):
    return lax.dot_general(a, b, dims(lhs, rhs), preferred_element_type=F32)


def kernel(
    fields_h, adj_h, couple_h, tmat_h, nbr_h, cls_h, fwd_ref, adjo_ref,
    fields, adj, nbr, cls, rows_w, slab, cols_w, mask, t_all,
    edge_f, edge_a, edge_c, fh_all, ah, clsh, expanded, part, landed, coup_all, s_all,
    load_sem, t_send, t_recv, tc_send, tc_recv, e_send, e_recv,
    f_send, f_recv, p_send, p_recv, c_send, c_recv, s_send, s_recv,
):
    rows, width = fields.shape
    wide = ah.shape[1]
    t, c = lax.axis_index("tiles"), lax.axis_index("coef")
    n_t, n_c = 16, 16
    mate = t + 1 - 2 * lax.rem(t, 2)

    def tile_at(step):
        return lax.rem(t + step, n_t)

    def coef_at(step):
        return lax.rem(c + step, n_c)

    own = pl.ds(pl.multiple_of(c * rows, rows), rows)
    lane0 = pl.multiple_of((c // 8) * LANE, LANE)

    loads = [
        pltpu.make_async_copy(fields_h, fields, load_sem.at[0]),
        pltpu.make_async_copy(adj_h, adj, load_sem.at[1]),
        pltpu.make_async_copy(tmat_h, t_all.at[pl.ds(t * 4, 4)], load_sem.at[2]),
        pltpu.make_async_copy(cls_h, cls, load_sem.at[3]),
        pltpu.make_async_copy(nbr_h, nbr, load_sem.at[4]),
        pltpu.make_async_copy(couple_h.at[:, :, pl.ds(lane0, LANE)], slab, load_sem.at[5]),
        pltpu.make_async_copy(couple_h.at[:, own, :], rows_w, load_sem.at[6]),
    ]
    for load in loads:
        load.start()

    barrier = pltpu.get_barrier_semaphore()
    for step in (1, 15, 2, 4, 6, 8, 10, 12, 14):
        pl.semaphore_signal(barrier, inc=1, device_id=(tile_at(step), c), device_id_type=MESH)
    for step in range(1, n_c):
        pl.semaphore_signal(barrier, inc=1, device_id=(t, coef_at(step)), device_id_type=MESH)
    for load in loads[:4]:
        load.wait()
    pl.semaphore_wait(barrier, 9 + n_c - 1)

    def remote(src, dst, send, recv, tile, coef):
        return pltpu.make_async_remote_copy(
            src_ref=src, dst_ref=dst, send_sem=send, recv_sem=recv,
            device_id=(tile, coef), device_id_type=MESH,
        )

    def shard(tile):
        return t_all.at[pl.ds(tile * 4, 4)]

    t_copies = [
        remote(shard(t), shard(t), t_send.at[s], t_recv.at[s], tile_at(2 * s), c) for s in range(1, 8)
    ]
    mate_copies = [remote(shard(t), shard(t), tc_send.at[0], tc_recv.at[0], mate, c)]
    for s in (4, 3, 5, 2, 6, 1, 7):
        t_copies[s - 1].start()
    first, last = pl.ds(0, LANE), pl.ds(width - LANE, LANE)
    edges = []
    for k, (src, dst) in enumerate(((adj, edge_a), (cls, edge_c), (fields, edge_f))):
        edges.append(remote(src.at[:, first], dst.at[0], e_send.at[2 * k], e_recv.at[2 * k], tile_at(15), c))
        edges.append(remote(src.at[:, last], dst.at[1], e_send.at[2 * k + 1], e_recv.at[2 * k + 1], tile_at(1), c))
    for edge in edges:
        edge.start()
    mate_copies[0].start()

    loads[4].wait()
    eye = (
        lax.broadcasted_iota(jnp.int32, (32, SLOTS), 0) == lax.broadcasted_iota(jnp.int32, (32, SLOTS), 1)
    ).astype(F32).astype(BF16)
    linked = (nbr[...] >= 0).astype(F32).astype(BF16)
    mask[...] = dot(eye, linked, 1, 1)

    ah[:, :width] = adj[...]
    clsh[:, :width] = cls[...]
    fh_all[own, :width] = fields[...]
    for edge in edges:
        edge.wait_recv()
    low = lax.broadcasted_iota(jnp.int32, (rows, LANE), 1) < LANE // 2
    low_row = lax.broadcasted_iota(jnp.int32, (1, LANE), 1) < LANE // 2
    ah[:, width:] = jnp.where(low, edge_a[0], edge_a[1])
    clsh[:, width:] = jnp.where(low_row, edge_c[0], edge_c[1])
    fh_all[own, width:] = jnp.where(low, edge_f[0], edge_f[1])

    order = (10, 6, 9, 11, 5, 7, 2, 14, 8, 13, 3, 1, 15, 4, 12)
    f_copies = {
        s: remote(fh_all.at[own], fh_all.at[own], f_send.at[s], f_recv.at[s], t, coef_at(s)) for s in order
    }
    for s in order:
        f_copies[s].start()

    adj_f = ah[...].astype(F32)
    cls_rows = jnp.broadcast_to(clsh[...], (rows, wide))
    for k in range(64):
        expanded[k * rows : (k + 1) * rows, :] = jnp.where(cls_rows == k, adj_f, 0.0).astype(BF16)

    loads[5].wait()
    loads[6].wait()
    pick = (
        lax.broadcasted_iota(jnp.int32, (rows, LANE), 1)
        == lax.broadcasted_iota(jnp.int32, (rows, LANE), 0) + lax.rem(c, 8) * rows
    ).astype(F32).astype(BF16)
    for m in range(SLOTS):
        cols_w[m] = dot(pick, slab[SLOTS - 1 - m], 1, 1).astype(BF16)

    for s in (1, 7, 2, 6, 3, 5, 4):
        t_copies[s - 1].wait_recv()
        came = tile_at(16 - 2 * s)
        passed = remote(shard(came), shard(came), tc_send.at[s], tc_recv.at[s], mate, c)
        passed.start()
        mate_copies.append(passed)
    for copy in mate_copies:
        copy.wait_recv()

    t_rows = t_all[...].reshape(64 * rows, 256)
    part[...] = dot(t_rows, expanded[...], 0, 0).astype(BF16)
    p_copies = {}
    for s in order:
        block = pl.ds(pl.multiple_of(coef_at(s) * rows, rows), rows)
        p_copies[s] = remote(part.at[block], landed.at[s], p_send.at[s], p_recv.at[s], t, coef_at(s))
        p_copies[s].start()

    def coupling(weights, source):
        product = dot(weights, source)
        total = jnp.zeros((rows, width), F32)
        for m in range(SLOTS):
            shift = m - HW + (1 if m >= HW else 0)
            rolled = pltpu.roll(product[m * rows : (m + 1) * rows], (-shift) % wide, 1)
            total += rolled[:, :width] * mask[m : m + 1, :]
        return total

    for s in order:
        f_copies[s].wait_recv()
    coup_all[own, :] = coupling(rows_w[...].reshape(SLOTS * rows, 256), fh_all[...]).astype(BF16)
    c_copies = {
        s: remote(coup_all.at[own], coup_all.at[own], c_send.at[s], c_recv.at[s], t, coef_at(s)) for s in order
    }
    for s in order:
        c_copies[s].start()

    total = part[own, :].astype(F32)
    for s in order:
        p_copies[s].wait_recv()
        total += landed[s].astype(F32)
    s_all[own, :] = total.astype(BF16)
    s_copies = {
        s: remote(s_all.at[own], s_all.at[own], s_send.at[s], s_recv.at[s], t, coef_at(s)) for s in order
    }
    for s in order:
        s_copies[s].start()

    for s in order:
        c_copies[s].wait_recv()
    cls_own = jnp.broadcast_to(cls[...], (rows, width))
    applied = jnp.zeros((rows, width), F32)
    for b in range(4):
        product = dot(t_all[16 * b : 16 * b + 16].reshape(16 * rows, 256), coup_all[...])
        for k in range(16):
            applied += jnp.where(cls_own == 16 * b + k, product[k * rows : (k + 1) * rows], 0.0)
    fwd_ref[...] = (fields[...].astype(F32) - applied).astype(BF16)

    for s in order:
        s_copies[s].wait_recv()
    returned = coupling(cols_w[...].reshape(SLOTS * rows, 256), s_all[...])
    adjo_ref[...] = (adj[...].astype(F32) - returned).astype(BF16)

    for copy in t_copies + mate_copies + edges:
        copy.wait_send()
    for group in (f_copies, p_copies, c_copies, s_copies):
        for s in order:
            group[s].wait_send()


def local(fields, adjoints, couple, tmatrices, neighbours, classes):
    rows, width = fields.shape
    wide = width + LANE
    kr = couple.shape[1]
    dma = pltpu.SemaphoreType.DMA
    anywhere = pl.BlockSpec(memory_space=pl.ANY)
    vmem = pl.BlockSpec(memory_space=pltpu.VMEM)
    return pl.pallas_call(
        kernel,
        out_shape=(jax.ShapeDtypeStruct((rows, width), BF16),) * 2,
        in_specs=[anywhere] * 6,
        out_specs=(vmem, vmem),
        scratch_shapes=[
            pltpu.VMEM((rows, width), BF16),
            pltpu.VMEM((rows, width), BF16),
            pltpu.VMEM((width, SLOTS), jnp.int32),
            pltpu.VMEM((1, width), jnp.int32),
            pltpu.VMEM((SLOTS, rows, kr), BF16),
            pltpu.VMEM((SLOTS, kr, LANE), BF16),
            pltpu.VMEM((SLOTS, rows, kr), BF16),
            pltpu.VMEM((32, width), F32),
            pltpu.VMEM((64, rows, kr), BF16),
            pltpu.VMEM((2, rows, LANE), BF16),
            pltpu.VMEM((2, rows, LANE), BF16),
            pltpu.VMEM((2, 1, LANE), jnp.int32),
            pltpu.VMEM((kr, wide), BF16),
            pltpu.VMEM((rows, wide), BF16),
            pltpu.VMEM((1, wide), jnp.int32),
            pltpu.VMEM((64 * rows, wide), BF16),
            pltpu.VMEM((kr, wide), BF16),
            pltpu.VMEM((16, rows, wide), BF16),
            pltpu.VMEM((kr, width), BF16),
            pltpu.VMEM((kr, wide), BF16),
            dma((7,)), dma((8,)), dma((8,)), dma((8,)), dma((8,)), dma((6,)), dma((6,)),
            dma((16,)), dma((16,)), dma((16,)), dma((16,)), dma((16,)), dma((16,)), dma((16,)), dma((16,)),
        ],
        compiler_params=pltpu.CompilerParams(
            collective_id=0, has_side_effects=True, vmem_limit_bytes=48 * 1024 * 1024
        ),
    )(fields, adjoints, couple, tmatrices, neighbours, classes.reshape(1, width))


def solution(mesh):
    placed = (
        P("coef", "tiles"),
        P("coef", "tiles"),
        P(),
        P("tiles", "coef", None),
        P("tiles", None),
        P("tiles"),
    )
    return jax.shard_map(
        local,
        mesh=mesh,
        in_specs=placed,
        out_specs=(P("coef", "tiles"), P("coef", "tiles")),
        check_vma=False,
    )
```

```python
import functools

import jax
import jax.numpy as jnp
from jax import lax
from jax.experimental import pallas as pl
from jax.experimental.pallas import tpu as pltpu
from jax.sharding import PartitionSpec as P

SLOTS = 30
HW = 15
LANE = 128
MESH = pl.DeviceIdType.MESH
F32 = jnp.float32
BF16 = jnp.bfloat16


def dims(lhs, rhs):
    return (((lhs,), (rhs,)), ((), ()))


def dot(a, b, lhs=1, rhs=0):
    return lax.dot_general(a, b, dims(lhs, rhs), preferred_element_type=F32)


def kernel(
    fields_h, adj_h, couple_h, tmat_h, nbr_h, cls_h, fwd_ref, adjo_ref,
    fields, adj, nbr, cls, rows_w, slab, cols_w, mask, t_all,
    edge_f, edge_a, edge_c, fh_all, ah, clsh, expanded, part, landed, coup_all, s_all,
    load_sem, t_send, t_recv, tc_send, tc_recv, e_send, e_recv,
    f_send, f_recv, p_send, p_recv, c_send, c_recv, s_send, s_recv,
):
    rows, width = fields.shape
    wide = ah.shape[1]
    t, c = lax.axis_index("tiles"), lax.axis_index("coef")
    n_t, n_c = 16, 16
    mate = t + 1 - 2 * lax.rem(t, 2)

    def tile_at(step):
        return lax.rem(t + step, n_t)

    def coef_at(step):
        return lax.rem(c + step, n_c)

    def peer(dx, dz):
        return lax.rem(c // 4 + dx, 4) * 4 + lax.rem(lax.rem(c, 4) + dz, 4)

    own = pl.ds(pl.multiple_of(c * rows, rows), rows)
    lane0 = pl.multiple_of((c // 8) * LANE, LANE)

    loads = [
        pltpu.make_async_copy(fields_h, fields, load_sem.at[0]),
        pltpu.make_async_copy(adj_h, adj, load_sem.at[1]),
        pltpu.make_async_copy(tmat_h, t_all.at[pl.ds(t * 4, 4)], load_sem.at[2]),
        pltpu.make_async_copy(cls_h, cls, load_sem.at[3]),
        pltpu.make_async_copy(nbr_h, nbr, load_sem.at[4]),
        pltpu.make_async_copy(couple_h.at[:, :, pl.ds(lane0, LANE)], slab, load_sem.at[5]),
        pltpu.make_async_copy(couple_h.at[:, own, :], rows_w, load_sem.at[6]),
    ]
    for load in loads:
        load.start()

    barrier = pltpu.get_barrier_semaphore()
    for step in (1, 15, 2, 4, 6, 8, 10, 12, 14):
        pl.semaphore_signal(barrier, inc=1, device_id=(tile_at(step), c), device_id_type=MESH)
    for step in range(1, n_c):
        pl.semaphore_signal(barrier, inc=1, device_id=(t, coef_at(step)), device_id_type=MESH)
    for load in loads[:4]:
        load.wait()
    pl.semaphore_wait(barrier, 9 + n_c - 1)

    def remote(src, dst, send, recv, tile, coef):
        return pltpu.make_async_remote_copy(
            src_ref=src, dst_ref=dst, send_sem=send, recv_sem=recv,
            device_id=(tile, coef), device_id_type=MESH,
        )

    def shard(tile):
        return t_all.at[pl.ds(tile * 4, 4)]

    class Gather:
        def __init__(self, buf, send, recv):
            self.copies = {}
            self.buf, self.send, self.recv = buf, send, recv

        def start(self, source, dx, dz, slot):
            block = self.buf.at[pl.ds(pl.multiple_of(source * rows, rows), rows)]
            copy = remote(block, block, self.send.at[slot], self.recv.at[slot], t, peer(dx, dz))
            copy.start()
            self.copies[slot] = copy

        def begin(self):
            for dz in (2, 1, 3):
                self.start(c, 0, dz, dz)
            for dx in (2, 1, 3):
                self.start(c, dx, 0, 4 * dx)

        def relay(self, dz):
            self.copies[dz].wait_recv()
            for dx in (2, 1, 3):
                self.start(peer(0, 4 - dz), dx, 0, 4 * dx + dz)

        def finish(self):
            for dz in (0, 1, 3, 2):
                for dx in (1, 3, 2):
                    self.copies[4 * dx + dz].wait_recv()

        def drain(self):
            for copy in self.copies.values():
                copy.wait_send()

    gather_f = Gather(fh_all, f_send, f_recv)
    gather_c = Gather(coup_all, c_send, c_recv)
    gather_s = Gather(s_all, s_send, s_recv)

    t_copies = [
        remote(shard(t), shard(t), t_send.at[s], t_recv.at[s], tile_at(2 * s), c) for s in range(1, 8)
    ]
    mate_copies = [remote(shard(t), shard(t), tc_send.at[0], tc_recv.at[0], mate, c)]
    for s in (4, 3, 5, 2, 6, 1, 7):
        t_copies[s - 1].start()
    first, last = pl.ds(0, LANE), pl.ds(width - LANE, LANE)
    edges = []
    for k, (src, dst) in enumerate(((adj, edge_a), (cls, edge_c), (fields, edge_f))):
        edges.append(remote(src.at[:, first], dst.at[0], e_send.at[2 * k], e_recv.at[2 * k], tile_at(15), c))
        edges.append(remote(src.at[:, last], dst.at[1], e_send.at[2 * k + 1], e_recv.at[2 * k + 1], tile_at(1), c))
    for edge in edges:
        edge.start()
    mate_copies[0].start()

    loads[4].wait()
    mask[...] = (nbr[...] >= 0).astype(F32)

    ah[:, :width] = adj[...]
    clsh[:, :width] = cls[...]
    fh_all[own, :width] = fields[...]
    for edge in edges:
        edge.wait_recv()
    low = lax.broadcasted_iota(jnp.int32, (rows, LANE), 1) < LANE // 2
    low_row = lax.broadcasted_iota(jnp.int32, (1, LANE), 1) < LANE // 2
    ah[:, width:] = jnp.where(low, edge_a[0], edge_a[1])
    clsh[:, width:] = jnp.where(low_row, edge_c[0], edge_c[1])
    fh_all[own, width:] = jnp.where(low, edge_f[0], edge_f[1])

    gather_f.begin()

    adj_f = ah[...].astype(F32)
    cls_rows = jnp.broadcast_to(clsh[...], (rows, wide))
    for k in range(64):
        expanded[k * rows : (k + 1) * rows, :] = jnp.where(cls_rows == k, adj_f, 0.0).astype(BF16)

    loads[5].wait()
    loads[6].wait()
    pick = (
        lax.broadcasted_iota(jnp.int32, (rows, LANE), 1)
        == lax.broadcasted_iota(jnp.int32, (rows, LANE), 0) + lax.rem(c, 8) * rows
    ).astype(F32).astype(BF16)
    for m in range(SLOTS):
        cols_w[m] = dot(pick, slab[SLOTS - 1 - m], 1, 1).astype(BF16)

    for s in (1, 7, 2, 6, 3, 5, 4):
        t_copies[s - 1].wait_recv()
        came = tile_at(16 - 2 * s)
        passed = remote(shard(came), shard(came), tc_send.at[s], tc_recv.at[s], mate, c)
        passed.start()
        mate_copies.append(passed)
    for copy in mate_copies:
        copy.wait_recv()

    t_rows = t_all[...].reshape(64 * rows, 256)
    part[...] = dot(t_rows, expanded[...], 0, 0).astype(BF16)
    p_copies = []
    for dx, dz in ((2, 2), (2, 1), (2, 3), (1, 2), (3, 2), (0, 2), (1, 1), (3, 1), (1, 3), (3, 3), (0, 1), (0, 3), (2, 0), (1, 0), (3, 0)):
        to, slot = peer(dx, dz), 4 * dx + dz
        block = pl.ds(pl.multiple_of(to * rows, rows), rows)
        p_copies.append(remote(part.at[block], landed.at[slot], p_send.at[slot], p_recv.at[slot], t, to))
        p_copies[-1].start()
    for dz in (1, 3, 2):
        gather_f.relay(dz)

    def coupling(weights, source):
        product = dot(weights, source)
        total = jnp.zeros((rows, width), F32)
        for m in range(SLOTS):
            shift = m - HW + (1 if m >= HW else 0)
            rolled = pltpu.roll(product[m * rows : (m + 1) * rows], (-shift) % wide, 1)
            total += rolled[:, :width] * mask[m : m + 1, :]
        return total

    gather_f.finish()
    coup_all[own, :] = coupling(rows_w[...].reshape(SLOTS * rows, 256), fh_all[...]).astype(BF16)
    gather_c.begin()

    total = part[own, :].astype(F32)
    for copy in p_copies[::-1]:
        copy.wait_recv()
    for slot in range(1, 16):
        total += landed[slot].astype(F32)
    s_all[own, :] = total.astype(BF16)
    gather_s.begin()
    for dz in (1, 3, 2):
        gather_c.relay(dz)
    for dz in (1, 3, 2):
        gather_s.relay(dz)

    gather_c.finish()
    cls_own = jnp.broadcast_to(cls[...], (rows, width))
    applied = jnp.zeros((rows, width), F32)
    for b in range(4):
        product = dot(t_all[16 * b : 16 * b + 16].reshape(16 * rows, 256), coup_all[...])
        for k in range(16):
            applied += jnp.where(cls_own == 16 * b + k, product[k * rows : (k + 1) * rows], 0.0)
    fwd_ref[...] = (fields[...].astype(F32) - applied).astype(BF16)

    gather_s.finish()
    returned = coupling(cols_w[...].reshape(SLOTS * rows, 256), s_all[...])
    adjo_ref[...] = (adj[...].astype(F32) - returned).astype(BF16)

    for copy in t_copies + mate_copies + edges + p_copies:
        copy.wait_send()
    for gather in (gather_f, gather_c, gather_s):
        gather.drain()


def local(fields, adjoints, couple, tmatrices, neighbours, classes):
    rows, width = fields.shape
    wide = width + LANE
    kr = couple.shape[1]
    dma = pltpu.SemaphoreType.DMA
    anywhere = pl.BlockSpec(memory_space=pl.ANY)
    vmem = pl.BlockSpec(memory_space=pltpu.VMEM)
    return pl.pallas_call(
        kernel,
        out_shape=(jax.ShapeDtypeStruct((rows, width), BF16),) * 2,
        in_specs=[anywhere] * 6,
        out_specs=(vmem, vmem),
        scratch_shapes=[
            pltpu.VMEM((rows, width), BF16),
            pltpu.VMEM((rows, width), BF16),
            pltpu.VMEM((SLOTS, width), jnp.int32),
            pltpu.VMEM((1, width), jnp.int32),
            pltpu.VMEM((SLOTS, rows, kr), BF16),
            pltpu.VMEM((SLOTS, kr, LANE), BF16),
            pltpu.VMEM((SLOTS, rows, kr), BF16),
            pltpu.VMEM((SLOTS, width), F32),
            pltpu.VMEM((64, rows, kr), BF16),
            pltpu.VMEM((2, rows, LANE), BF16),
            pltpu.VMEM((2, rows, LANE), BF16),
            pltpu.VMEM((2, 1, LANE), jnp.int32),
            pltpu.VMEM((kr, wide), BF16),
            pltpu.VMEM((rows, wide), BF16),
            pltpu.VMEM((1, wide), jnp.int32),
            pltpu.VMEM((64 * rows, wide), BF16),
            pltpu.VMEM((kr, wide), BF16),
            pltpu.VMEM((16, rows, wide), BF16),
            pltpu.VMEM((kr, width), BF16),
            pltpu.VMEM((kr, wide), BF16),
            dma((7,)), dma((8,)), dma((8,)), dma((8,)), dma((8,)), dma((6,)), dma((6,)),
            dma((16,)), dma((16,)), dma((16,)), dma((16,)), dma((16,)), dma((16,)), dma((16,)), dma((16,)),
        ],
        compiler_params=pltpu.CompilerParams(
            collective_id=0, has_side_effects=True, vmem_limit_bytes=62 * 1024 * 1024
        ),
    )(fields, adjoints, couple, tmatrices, neighbours.T, classes.reshape(1, width))


def solution(mesh):
    placed = (
        P("coef", "tiles"),
        P("coef", "tiles"),
        P(),
        P("tiles", "coef", None),
        P("tiles", None),
        P("tiles"),
    )
    return jax.shard_map(
        local,
        mesh=mesh,
        in_specs=placed,
        out_specs=(P("coef", "tiles"), P("coef", "tiles")),
        check_vma=False,
    )
```

```python
import jax
import jax.numpy as jnp
from jax import lax
from jax.experimental import pallas as pl
from jax.experimental.pallas import tpu as pltpu
from jax.sharding import PartitionSpec as P

SLOTS = 30
HW = 15
LANE = 128
MESH = pl.DeviceIdType.MESH
F32 = jnp.float32
BF16 = jnp.bfloat16


def dot(a, b, lhs=1, rhs=0):
    return lax.dot_general(a, b, (((lhs,), (rhs,)), ((), ())), preferred_element_type=F32)


def kernel(
    fields_h, adj_h, couple_h, tmat_h, nbr_h, cls_h, fwd_ref, adjo_ref,
    fields, adj, nbr, cls, rows_w, slab, cols_w, mask, t_all, tt_src, by_x, by_z, tt_all,
    edge_f, edge_a, edge_c, f_all, a_all, clsh, expanded, coup_all, s_all,
    load_sem, t_send, t_recv, tm_send, tm_recv, u_send, u_recv, um_send, um_recv,
    x_send, x_recv, z_send, z_recv, e_send, e_recv,
    f_send, f_recv, a_send, a_recv, c_send, c_recv, s_send, s_recv, z_known,
):
    rows, width = fields.shape
    wide = a_all.shape[1]
    t, c = lax.axis_index("tiles"), lax.axis_index("coef")
    x, z = c // 4, lax.rem(c, 4)
    mate = t + 1 - 2 * lax.rem(t, 2)

    def tile_at(step):
        return lax.rem(t + step, 16)

    def peer(dx, dz):
        return lax.rem(x + dx, 4) * 4 + lax.rem(z + dz, 4)

    def span(index, size):
        return pl.ds(pl.multiple_of(index * size, size), size)

    own = span(c, rows)
    lanes = span(c // 8, LANE)

    loads = [
        pltpu.make_async_copy(tmat_h, t_all.at[span(t, 4)], load_sem.at[0]),
        pltpu.make_async_copy(adj_h, adj, load_sem.at[1]),
        pltpu.make_async_copy(fields_h, fields, load_sem.at[2]),
        pltpu.make_async_copy(cls_h, cls, load_sem.at[3]),
        pltpu.make_async_copy(nbr_h, nbr, load_sem.at[4]),
        pltpu.make_async_copy(couple_h.at[:, :, lanes], slab, load_sem.at[5]),
        pltpu.make_async_copy(couple_h.at[:, own, :], rows_w, load_sem.at[6]),
    ]
    for load in loads:
        load.start()

    barrier = pltpu.get_barrier_semaphore()
    near_tiles, near_coef = (1, 15, 2, 4, 6, 8, 10, 12, 14), ((1, 0), (2, 0), (3, 0), (0, 1), (0, 3))
    for step in near_tiles:
        pl.semaphore_signal(barrier, inc=1, device_id=(tile_at(step), c), device_id_type=MESH)
    for dx, dz in near_coef:
        pl.semaphore_signal(barrier, inc=1, device_id=(t, peer(dx, dz)), device_id_type=MESH)
    for load in loads[:4]:
        load.wait()
    flat = t_all[span(t, 4)].reshape(4 * rows, 256)
    tt_src[...] = jnp.concatenate([flat, flat], axis=0).T
    pl.semaphore_wait(barrier, len(near_tiles) + len(near_coef))
    pl.semaphore_signal(z_known, inc=1, device_id=(t, peer(0, 1)), device_id_type=MESH)

    def remote(src, dst, send, recv, tile, coef):
        copy = pltpu.make_async_remote_copy(
            src_ref=src, dst_ref=dst, send_sem=send, recv_sem=recv,
            device_id=(tile, coef), device_id_type=MESH,
        )
        copy.start()
        return copy

    x_copies = [
        remote(tt_src.at[span(lax.rem(x + dx, 4), 64)], by_x.at[x], x_send.at[dx], x_recv.at[dx], t, peer(dx, 0))
        for dx in (2, 1, 3)
    ]
    edges = []
    for k, (src, dst) in enumerate(((adj, edge_a), (fields, edge_f), (cls, edge_c))):
        for side, (start, step) in enumerate(((0, 15), (width - LANE, 1))):
            slot = 2 * k + side
            edges.append(
                remote(src.at[:, pl.ds(start, LANE)], dst.at[side], e_send.at[slot], e_recv.at[slot], tile_at(step), c)
            )

    class Spread:
        def __init__(self, buf, size, send, recv, mate_send, mate_recv):
            self.buf, self.size = buf, size
            self.mate_send, self.mate_recv = mate_send, mate_recv
            mine = self.shard(t)
            self.copies = {s: remote(mine, mine, send.at[s], recv.at[s], tile_at(2 * s), c) for s in (4, 3, 5, 2, 6, 1, 7)}
            self.passed = [remote(mine, mine, mate_send.at[0], mate_recv.at[0], mate, c)]

        def shard(self, tile):
            return self.buf.at[span(tile, self.size)]

        def pass_on(self):
            for s in (1, 7, 2, 6, 3, 5, 4):
                self.copies[s].wait_recv()
                came = self.shard(tile_at(16 - 2 * s))
                self.passed.append(remote(came, came, self.mate_send.at[s], self.mate_recv.at[s], mate, c))

        def finish(self):
            for copy in self.passed:
                copy.wait_recv()

        def drain(self):
            for copy in list(self.copies.values()) + self.passed:
                copy.wait_send()

    class Gather:
        def __init__(self, buf, send, recv):
            self.copies = {}
            self.buf, self.send, self.recv = buf, send, recv

        def start(self, source, dx, dz, slot):
            block = self.buf.at[span(source, rows)]
            self.copies[slot] = remote(block, block, self.send.at[slot], self.recv.at[slot], t, peer(dx, dz))

        def begin(self):
            for dz in (2, 1, 3):
                self.start(c, 0, dz, dz)
            for dx in (2, 1, 3):
                self.start(c, dx, 0, 4 * dx)

        def relay(self):
            for dz in (1, 3, 2):
                self.copies[dz].wait_recv()
                for dx in (2, 1, 3):
                    self.start(peer(0, 4 - dz), dx, 0, 4 * dx + dz)

        def finish(self):
            for dz in (0, 1, 3, 2):
                for dx in (1, 3, 2):
                    self.copies[4 * dx + dz].wait_recv()

        def drain(self):
            for copy in self.copies.values():
                copy.wait_send()

    gather_f = Gather(f_all, f_send, f_recv)
    gather_a = Gather(a_all, a_send, a_recv)
    gather_c = Gather(coup_all, c_send, c_recv)
    gather_s = Gather(s_all, s_send, s_recv)

    t_rows = Spread(t_all, 4, t_send, t_recv, tm_send, tm_recv)

    by_x[x] = tt_src[span(x, 64)]
    a_all[own, :width] = adj[...]
    f_all[own, :width] = fields[...]
    clsh[:, :width] = cls[...]
    for copy in x_copies:
        copy.wait_recv()
    pl.semaphore_wait(z_known, 1)
    z_copies = [
        remote(by_x.at[:, span(lax.rem(z + dz, 4), rows), :], by_z.at[z], z_send.at[dz], z_recv.at[dz], t, peer(0, dz))
        for dz in (2, 1, 3)
    ]
    by_z[z] = by_x[:, span(z, rows), :]

    for edge in edges:
        edge.wait_recv()
    low = lax.broadcasted_iota(jnp.int32, (rows, LANE), 1) < LANE // 2
    low_row = lax.broadcasted_iota(jnp.int32, (1, LANE), 1) < LANE // 2
    a_all[own, width:] = jnp.where(low, edge_a[0], edge_a[1])
    f_all[own, width:] = jnp.where(low, edge_f[0], edge_f[1])
    clsh[:, width:] = jnp.where(low_row, edge_c[0], edge_c[1])
    gather_a.begin()
    gather_f.begin()

    loads[4].wait()
    mask[...] = (nbr[...] >= 0).astype(F32)
    loads[5].wait()
    loads[6].wait()
    pick = (
        lax.broadcasted_iota(jnp.int32, (rows, LANE), 1)
        == lax.broadcasted_iota(jnp.int32, (rows, LANE), 0) + lax.rem(c, 8) * rows
    ).astype(F32).astype(BF16)
    for m in range(SLOTS):
        cols_w[m] = dot(pick, slab[SLOTS - 1 - m], 1, 1).astype(BF16)

    t_rows.pass_on()
    for copy in z_copies:
        copy.wait_recv()
    for source_z in range(4):
        for half in range(2):
            block = jnp.where(low, by_z[source_z, 2 * half], by_z[source_z, 2 * half + 1])
            tt_all[span(t, rows), pl.ds((2 * source_z + half) * LANE, LANE)] = block
    t_cols = Spread(tt_all, rows, u_send, u_recv, um_send, um_recv)

    gather_a.relay()
    gather_f.relay()
    gather_a.finish()
    within = jnp.broadcast_to(jnp.bitwise_and(clsh[...], 3), (rows, wide))
    for source_z in range(4):
        for source_x in range(4):
            source = 4 * source_x + source_z
            values = a_all[source * rows : (source + 1) * rows].astype(F32)
            for k in range(4):
                at = ((4 * source_z + source_x) * 4 + k) * rows
                expanded[at : at + rows, :] = jnp.where(within == k, values, 0.0).astype(BF16)

    def coupling(weights, source):
        product = dot(weights, source)
        total = jnp.zeros((rows, width), F32)
        for m in range(SLOTS):
            shift = m - HW + (1 if m >= HW else 0)
            rolled = pltpu.roll(product[m * rows : (m + 1) * rows], (-shift) % wide, 1)
            total += rolled[:, :width] * mask[m : m + 1, :]
        return total

    gather_f.finish()
    coup_all[own, :] = coupling(rows_w[...].reshape(SLOTS * rows, 256), f_all[...]).astype(BF16)
    gather_c.begin()

    t_cols.pass_on()
    t_cols.finish()
    product = dot(tt_all[...], expanded[...])
    group = jnp.broadcast_to(lax.shift_right_arithmetic(clsh[...], jnp.full((1, wide), 2, jnp.int32)), (rows, wide))
    scattered = jnp.zeros((rows, wide), F32)
    for k in range(16):
        scattered += jnp.where(group == k, product[k * rows : (k + 1) * rows], 0.0)
    s_all[own, :] = scattered.astype(BF16)
    gather_s.begin()
    gather_c.relay()
    gather_s.relay()

    t_rows.finish()
    gather_c.finish()
    cls_own = jnp.broadcast_to(cls[...], (rows, width))
    applied = jnp.zeros((rows, width), F32)
    for b in range(4):
        product = dot(t_all[16 * b : 16 * b + 16].reshape(16 * rows, 256), coup_all[...])
        for k in range(16):
            applied += jnp.where(cls_own == 16 * b + k, product[k * rows : (k + 1) * rows], 0.0)
    fwd_ref[...] = (fields[...].astype(F32) - applied).astype(BF16)

    gather_s.finish()
    returned = coupling(cols_w[...].reshape(SLOTS * rows, 256), s_all[...])
    adjo_ref[...] = (adj[...].astype(F32) - returned).astype(BF16)

    for copy in x_copies + z_copies + edges:
        copy.wait_send()
    for group_copies in (t_rows, t_cols, gather_f, gather_a, gather_c, gather_s):
        group_copies.drain()


def hand_over(fwd_ref, adj_ref, fwd_out, adj_out, sem):
    copies = [
        pltpu.make_async_copy(fwd_ref, fwd_out, sem.at[0]),
        pltpu.make_async_copy(adj_ref, adj_out, sem.at[1]),
    ]
    for copy in copies:
        copy.start()
    for copy in copies:
        copy.wait()


def local(fields, adjoints, couple, tmatrices, neighbours, classes):
    rows, width = fields.shape
    wide = width + LANE
    kr = couple.shape[1]
    dma = pltpu.SemaphoreType.DMA
    anywhere = pl.BlockSpec(memory_space=pl.ANY)
    vmem = pl.BlockSpec(memory_space=pltpu.VMEM)
    outputs = (jax.ShapeDtypeStruct((rows, width), BF16),) * 2
    operands = (fields, adjoints, couple, tmatrices, neighbours.T, classes.reshape(1, width))
    results = pl.pallas_call(
        kernel,
        out_shape=outputs,
        in_specs=[anywhere] * 6,
        out_specs=(vmem, vmem),
        scratch_shapes=[
            pltpu.VMEM((rows, width), BF16),
            pltpu.VMEM((rows, width), BF16),
            pltpu.VMEM((SLOTS, width), jnp.int32),
            pltpu.VMEM((1, width), jnp.int32),
            pltpu.VMEM((SLOTS, rows, kr), BF16),
            pltpu.VMEM((SLOTS, kr, LANE), BF16),
            pltpu.VMEM((SLOTS, rows, kr), BF16),
            pltpu.VMEM((SLOTS, width), F32),
            pltpu.VMEM((64, rows, kr), BF16),
            pltpu.VMEM((kr, LANE), BF16),
            pltpu.VMEM((4, 64, LANE), BF16),
            pltpu.VMEM((4, 4, rows, LANE), BF16),
            pltpu.VMEM((kr, 1024), BF16),
            pltpu.VMEM((2, rows, LANE), BF16),
            pltpu.VMEM((2, rows, LANE), BF16),
            pltpu.VMEM((2, 1, LANE), jnp.int32),
            pltpu.VMEM((kr, wide), BF16),
            pltpu.VMEM((kr, wide), BF16),
            pltpu.VMEM((1, wide), jnp.int32),
            pltpu.VMEM((1024, wide), BF16),
            pltpu.VMEM((kr, width), BF16),
            pltpu.VMEM((kr, wide), BF16),
            dma((7,)),
        ]
        + [dma((8,))] * 8
        + [dma((4,))] * 4
        + [dma((6,))] * 2
        + [dma((16,))] * 8
        + [pltpu.SemaphoreType.REGULAR],
        compiler_params=pltpu.CompilerParams(
            collective_id=0, has_side_effects=True, vmem_limit_bytes=40 * 1024 * 1024
        ),
    )(*[pltpu.with_memory_space_constraint(v, pltpu.HBM) for v in operands])
    return pl.pallas_call(
        hand_over,
        out_shape=outputs,
        in_specs=[vmem, vmem],
        out_specs=(anywhere, anywhere),
        scratch_shapes=[dma((2,))],
        compiler_params=pltpu.CompilerParams(vmem_limit_bytes=1024 * 1024),
    )(*results)


def solution(mesh):
    placed = (
        P("coef", "tiles"),
        P("coef", "tiles"),
        P(),
        P("tiles", "coef", None),
        P("tiles", None),
        P("tiles"),
    )
    return jax.shard_map(
        local,
        mesh=mesh,
        in_specs=placed,
        out_specs=(P("coef", "tiles"), P("coef", "tiles")),
        check_vma=False,
    )
```

```python
import jax
import jax.numpy as jnp
from jax import lax
from jax.experimental import pallas as pl
from jax.experimental.pallas import tpu as pltpu
from jax.sharding import PartitionSpec as P

SLOTS = 30
HW = 15
LANE = 128
MESH = pl.DeviceIdType.MESH
F32 = jnp.float32
BF16 = jnp.bfloat16


def dot(a, b, lhs=1, rhs=0):
    return lax.dot_general(a, b, (((lhs,), (rhs,)), ((), ())), preferred_element_type=F32)


def kernel(
    fields_h, adj_h, couple_h, tmat_h, nbr_h, cls_h, fwd_ref, adjo_ref,
    fields, adj, nbr, cls, rows_w, slab, cols_w, mask, t_all, tt_src, by_x, by_z, tt_all,
    edge_f, edge_a, edge_c, af_all, ends_all, clsh, expanded, coup_all, s_all,
    load_sem, t_send, t_recv, tm_send, tm_recv, u_send, u_recv, um_send, um_recv,
    x_send, x_recv, z_send, z_recv, e_send, e_recv,
    g_send, g_recv, h_send, h_recv, c_send, c_recv, s_send, s_recv, z_known,
):
    rows, width = fields.shape
    wide = clsh.shape[1]
    t, c = lax.axis_index("tiles"), lax.axis_index("coef")
    x, z = c // 4, lax.rem(c, 4)
    mate = t + 1 - 2 * lax.rem(t, 2)

    def tile_at(step):
        return lax.rem(t + step, 16)

    def peer(dx, dz):
        return lax.rem(x + dx, 4) * 4 + lax.rem(z + dz, 4)

    def span(index, size):
        return pl.ds(pl.multiple_of(index * size, size), size)

    own = span(c, rows)
    lanes = span(c // 8, LANE)

    loads = [
        pltpu.make_async_copy(tmat_h, t_all.at[span(t, 4)], load_sem.at[0]),
        pltpu.make_async_copy(adj_h, adj, load_sem.at[1]),
        pltpu.make_async_copy(fields_h, fields, load_sem.at[2]),
        pltpu.make_async_copy(cls_h, cls, load_sem.at[3]),
        pltpu.make_async_copy(nbr_h, nbr, load_sem.at[4]),
        pltpu.make_async_copy(couple_h.at[:, :, lanes], slab, load_sem.at[5]),
        pltpu.make_async_copy(couple_h.at[:, own, :], rows_w, load_sem.at[6]),
    ]
    for load in loads:
        load.start()

    barrier = pltpu.get_barrier_semaphore()
    near_tiles, near_coef = (1, 15, 2, 4, 6, 8, 10, 12, 14), ((1, 0), (2, 0), (3, 0), (0, 1), (0, 3))
    for step in near_tiles:
        pl.semaphore_signal(barrier, inc=1, device_id=(tile_at(step), c), device_id_type=MESH)
    for dx, dz in near_coef:
        pl.semaphore_signal(barrier, inc=1, device_id=(t, peer(dx, dz)), device_id_type=MESH)
    for load in loads[:4]:
        load.wait()
    flat = t_all[span(t, 4)].reshape(4 * rows, 256)
    tt_src[...] = jnp.concatenate([flat, flat], axis=0).T
    af_all[own, :width] = adj[...]
    af_all[own, width:] = fields[...]
    pl.semaphore_wait(barrier, len(near_tiles) + len(near_coef))
    pl.semaphore_signal(z_known, inc=1, device_id=(t, peer(0, 1)), device_id_type=MESH)

    def remote(src, dst, send, recv, tile, coef):
        copy = pltpu.make_async_remote_copy(
            src_ref=src, dst_ref=dst, send_sem=send, recv_sem=recv,
            device_id=(tile, coef), device_id_type=MESH,
        )
        copy.start()
        return copy

    class Spread:
        def __init__(self, shard, first, send, recv, mate_send, mate_recv):
            self.shard, self.first = shard, first
            self.mate_send, self.mate_recv = mate_send, mate_recv
            mine = shard(t)
            self.copies = {
                s: remote(mine, mine, send.at[first + s], recv.at[first + s], tile_at(2 * s), c)
                for s in (4, 3, 5, 2, 6, 1, 7)
            }
            self.passed = [remote(mine, mine, mate_send.at[first], mate_recv.at[first], mate, c)]

        def pass_on(self):
            for s in (1, 7, 2, 6, 3, 5, 4):
                self.copies[s].wait_recv()
                came, slot = self.shard(tile_at(16 - 2 * s)), self.first + s
                self.passed.append(remote(came, came, self.mate_send.at[slot], self.mate_recv.at[slot], mate, c))

        def finish(self):
            for copy in self.passed:
                copy.wait_recv()

        def drain(self):
            for copy in list(self.copies.values()) + self.passed:
                copy.wait_send()

    class Gather:
        def __init__(self, buf, send, recv):
            self.copies = {}
            self.buf, self.send, self.recv = buf, send, recv

        def start(self, source, dx, dz, slot):
            block = self.buf.at[span(source, rows)]
            self.copies[slot] = remote(block, block, self.send.at[slot], self.recv.at[slot], t, peer(dx, dz))

        def along_z(self, *steps):
            for dz in steps:
                self.start(c, 0, dz, dz)

        def along_x(self):
            for dx in (2, 1, 3):
                self.start(c, dx, 0, 4 * dx)

        def begin(self):
            self.along_z(2, 1, 3)
            self.along_x()

        def relay(self, *steps):
            for dz in steps or (1, 3, 2):
                self.copies[dz].wait_recv()
                for dx in (2, 1, 3):
                    self.start(peer(0, 4 - dz), dx, 0, 4 * dx + dz)

        def finish(self):
            for dz in (0, 1, 3, 2):
                for dx in (1, 3, 2):
                    self.copies[4 * dx + dz].wait_recv()

        def drain(self):
            for copy in self.copies.values():
                copy.wait_send()

    gather = Gather(af_all, g_send, g_recv)
    gather_ends = Gather(ends_all, h_send, h_recv)
    gather_c = Gather(coup_all, c_send, c_recv)
    gather_s = Gather(s_all, s_send, s_recv)

    x_copies = [
        remote(tt_src.at[span(lax.rem(x + dx, 4), 64)], by_x.at[x], x_send.at[dx], x_recv.at[dx], t, peer(dx, 0))
        for dx in (2, 1, 3)
    ]
    edges = []
    for k, (src, dst) in enumerate(((adj, edge_a), (fields, edge_f), (cls, edge_c))):
        for side, (start, step) in enumerate(((0, 15), (width - LANE, 1))):
            slot = 2 * k + side
            edges.append(
                remote(src.at[:, pl.ds(start, LANE)], dst.at[side], e_send.at[slot], e_recv.at[slot], tile_at(step), c)
            )

    by_x[x] = tt_src[span(x, 64)]
    clsh[:, :width] = cls[...]
    gather.along_z(1, 3)
    gather.along_x()
    for copy in x_copies:
        copy.wait_recv()
    pl.semaphore_wait(z_known, 1)
    z_copies = {
        dz: remote(by_x.at[:, span(lax.rem(z + dz, 4), rows), :], by_z.at[z], z_send.at[dz], z_recv.at[dz], t, peer(0, dz))
        for dz in (2, 1, 3)
    }
    gather.along_z(2)
    by_z[z] = by_x[:, span(z, rows), :]
    low = lax.broadcasted_iota(jnp.int32, (rows, LANE), 1) < LANE // 2
    t_cols = {}

    def spread_quarter(dz):
        if dz:
            z_copies[dz].wait_recv()
        source_z = lax.rem(z + 4 - dz, 4)
        for half in range(2):
            block = jnp.where(low, by_z[source_z, 2 * half], by_z[source_z, 2 * half + 1])
            tt_all[source_z, span(t, rows), half * LANE : (half + 1) * LANE] = block
        t_cols[dz] = Spread(
            lambda tile: tt_all.at[source_z, span(tile, rows)], 8 * dz, u_send, u_recv, um_send, um_recv
        )

    spread_quarter(0)

    for edge in edges:
        edge.wait_recv()
    low_row = lax.broadcasted_iota(jnp.int32, (1, LANE), 1) < LANE // 2
    ends_all[own, :LANE] = jnp.where(low, edge_a[0], edge_a[1])
    ends_all[own, LANE:] = jnp.where(low, edge_f[0], edge_f[1])
    clsh[:, width:] = jnp.where(low_row, edge_c[0], edge_c[1])
    gather_ends.begin()
    gather.relay(1, 3)

    loads[4].wait()
    mask[...] = (nbr[...] >= 0).astype(F32)
    loads[5].wait()
    loads[6].wait()
    pick = (
        lax.broadcasted_iota(jnp.int32, (rows, LANE), 1)
        == lax.broadcasted_iota(jnp.int32, (rows, LANE), 0) + lax.rem(c, 8) * rows
    ).astype(F32).astype(BF16)
    for m in range(SLOTS):
        cols_w[m] = dot(pick, slab[SLOTS - 1 - m], 1, 1).astype(BF16)

    spread_quarter(1)
    spread_quarter(3)
    spread_quarter(2)
    t_rows = Spread(lambda tile: t_all.at[span(tile, 4)], 0, t_send, t_recv, tm_send, tm_recv)
    gather.relay(2)
    gather_ends.relay()

    def coupling(weights, inner, ends):
        product = jnp.concatenate([dot(weights, inner), dot(weights, ends)], axis=1)
        total = jnp.zeros((rows, width), F32)
        for m in range(SLOTS):
            shift = m - HW + (1 if m >= HW else 0)
            rolled = pltpu.roll(product[m * rows : (m + 1) * rows], (-shift) % wide, 1)
            total += rolled[:, :width] * mask[m : m + 1, :]
        return total

    for dz in (0, 1, 3):
        t_cols[dz].pass_on()
    gather.finish()
    within = jnp.broadcast_to(jnp.bitwise_and(clsh[...], 3), (rows, wide))
    for source_z in range(4):
        for source_x in range(4):
            source = 4 * source_x + source_z
            block = slice(source * rows, (source + 1) * rows)
            values = af_all[block, :width].astype(F32)
            for k in range(4):
                at = ((4 * source_z + source_x) * 4 + k) * rows
                expanded[at : at + rows, :width] = jnp.where(within[:, :width] == k, values, 0.0).astype(BF16)
    t_cols[2].pass_on()
    gather_ends.finish()
    own_rows = rows_w[...].reshape(SLOTS * rows, 256)
    coup_all[own, :] = coupling(own_rows, af_all[:, width:], ends_all[:, LANE:]).astype(BF16)
    gather_c.begin()

    for source_z in range(4):
        for source_x in range(4):
            source = 4 * source_x + source_z
            block = slice(source * rows, (source + 1) * rows)
            values = ends_all[block, :LANE].astype(F32)
            for k in range(4):
                at = ((4 * source_z + source_x) * 4 + k) * rows
                expanded[at : at + rows, width:] = jnp.where(within[:, width:] == k, values, 0.0).astype(BF16)
    product = jnp.zeros((256, wide), F32)
    for dz in (0, 1, 3, 2):
        t_cols[dz].finish()
        quarter = lax.rem(z + 4 - dz, 4)
        product += dot(tt_all[quarter], expanded[span(quarter, 256)])
    group = jnp.broadcast_to(lax.shift_right_arithmetic(clsh[...], jnp.full((1, wide), 2, jnp.int32)), (rows, wide))
    scattered = jnp.zeros((rows, wide), F32)
    for k in range(16):
        scattered += jnp.where(group == k, product[k * rows : (k + 1) * rows], 0.0)
    s_all[own, :] = scattered.astype(BF16)
    gather_s.begin()
    t_rows.pass_on()
    gather_c.relay()
    gather_s.relay()

    t_rows.finish()
    gather_c.finish()
    cls_own = jnp.broadcast_to(cls[...], (rows, width))
    applied = jnp.zeros((rows, width), F32)
    for b in range(4):
        product = dot(t_all[16 * b : 16 * b + 16].reshape(16 * rows, 256), coup_all[...])
        for k in range(16):
            applied += jnp.where(cls_own == 16 * b + k, product[k * rows : (k + 1) * rows], 0.0)
    fwd_ref[...] = (fields[...].astype(F32) - applied).astype(BF16)

    gather_s.finish()
    returned = coupling(cols_w[...].reshape(SLOTS * rows, 256), s_all[:, :width], s_all[:, width:])
    adjo_ref[...] = (adj[...].astype(F32) - returned).astype(BF16)

    for copy in x_copies + list(z_copies.values()) + edges:
        copy.wait_send()
    for group_copies in (t_rows, *t_cols.values(), gather, gather_ends, gather_c, gather_s):
        group_copies.drain()


def hand_over(fwd_ref, adj_ref, fwd_out, adj_out, sem):
    copies = [
        pltpu.make_async_copy(fwd_ref, fwd_out, sem.at[0]),
        pltpu.make_async_copy(adj_ref, adj_out, sem.at[1]),
    ]
    for copy in copies:
        copy.start()
    for copy in copies:
        copy.wait()


def local(fields, adjoints, couple, tmatrices, neighbours, classes):
    rows, width = fields.shape
    wide = width + LANE
    kr = couple.shape[1]
    dma = pltpu.SemaphoreType.DMA
    anywhere = pl.BlockSpec(memory_space=pl.ANY)
    vmem = pl.BlockSpec(memory_space=pltpu.VMEM)
    outputs = (jax.ShapeDtypeStruct((rows, width), BF16),) * 2
    operands = (fields, adjoints, couple, tmatrices, neighbours.T, classes.reshape(1, width))
    results = pl.pallas_call(
        kernel,
        out_shape=outputs,
        in_specs=[anywhere] * 6,
        out_specs=(vmem, vmem),
        scratch_shapes=[
            pltpu.VMEM((rows, width), BF16),
            pltpu.VMEM((rows, width), BF16),
            pltpu.VMEM((SLOTS, width), jnp.int32),
            pltpu.VMEM((1, width), jnp.int32),
            pltpu.VMEM((SLOTS, rows, kr), BF16),
            pltpu.VMEM((SLOTS, kr, LANE), BF16),
            pltpu.VMEM((SLOTS, rows, kr), BF16),
            pltpu.VMEM((SLOTS, width), F32),
            pltpu.VMEM((64, rows, kr), BF16),
            pltpu.VMEM((kr, LANE), BF16),
            pltpu.VMEM((4, 64, LANE), BF16),
            pltpu.VMEM((4, 4, rows, LANE), BF16),
            pltpu.VMEM((4, kr, 256), BF16),
            pltpu.VMEM((2, rows, LANE), BF16),
            pltpu.VMEM((2, rows, LANE), BF16),
            pltpu.VMEM((2, 1, LANE), jnp.int32),
            pltpu.VMEM((kr, 2 * width), BF16),
            pltpu.VMEM((kr, 2 * LANE), BF16),
            pltpu.VMEM((1, wide), jnp.int32),
            pltpu.VMEM((1024, wide), BF16),
            pltpu.VMEM((kr, width), BF16),
            pltpu.VMEM((kr, wide), BF16),
            dma((7,)),
        ]
        + [dma((8,))] * 4
        + [dma((32,))] * 4
        + [dma((4,))] * 4
        + [dma((6,))] * 2
        + [dma((16,))] * 8
        + [pltpu.SemaphoreType.REGULAR],
        compiler_params=pltpu.CompilerParams(
            collective_id=0, has_side_effects=True, vmem_limit_bytes=40 * 1024 * 1024
        ),
    )(*[pltpu.with_memory_space_constraint(v, pltpu.HBM) for v in operands])
    return pl.pallas_call(
        hand_over,
        out_shape=outputs,
        in_specs=[vmem, vmem],
        out_specs=(anywhere, anywhere),
        scratch_shapes=[dma((2,))],
        compiler_params=pltpu.CompilerParams(vmem_limit_bytes=1024 * 1024),
    )(*results)


def solution(mesh):
    placed = (
        P("coef", "tiles"),
        P("coef", "tiles"),
        P(),
        P("tiles", "coef", None),
        P("tiles", None),
        P("tiles"),
    )
    return jax.shard_map(
        local,
        mesh=mesh,
        in_specs=placed,
        out_specs=(P("coef", "tiles"), P("coef", "tiles")),
        check_vma=False,
    )
```

```python
import jax
import jax.numpy as jnp
from jax import lax
from jax.experimental import pallas as pl
from jax.experimental.pallas import tpu as pltpu
from jax.sharding import PartitionSpec as P

SLOTS = 30
HW = 15
LANE = 128
MESH = pl.DeviceIdType.MESH
F32 = jnp.float32
BF16 = jnp.bfloat16


def dot(a, b, lhs=1, rhs=0):
    return lax.dot_general(a, b, (((lhs,), (rhs,)), ((), ())), preferred_element_type=F32)


def kernel(
    fields_h, adj_h, couple_h, tmat_h, nbr_h, cls_h, fwd_ref, adjo_ref,
    fields, adj, nbr, cls, rows_w, slab, cols_w, mask, t_all, tt_src, by_x, by_z, tt_all,
    edge_f, edge_a, edge_c, af_all, ends_all, clsh, expanded, coup_all, s_all,
    load_sem, t_send, t_recv, tm_send, tm_recv, u_send, u_recv, um_send, um_recv,
    x_send, x_recv, z_send, z_recv, e_send, e_recv,
    g_send, g_recv, h_send, h_recv, c_send, c_recv, s_send, s_recv, z_known,
):
    rows, width = fields.shape
    wide = clsh.shape[1]
    t, c = lax.axis_index("tiles"), lax.axis_index("coef")
    x, z = c // 4, lax.rem(c, 4)
    mate = t + 1 - 2 * lax.rem(t, 2)

    def tile_at(step):
        return lax.rem(t + step, 16)

    def peer(dx, dz):
        return lax.rem(x + dx, 4) * 4 + lax.rem(z + dz, 4)

    def span(index, size):
        return pl.ds(pl.multiple_of(index * size, size), size)

    own = span(c, rows)
    lanes = span(c // 8, LANE)

    loads = [
        pltpu.make_async_copy(tmat_h, t_all.at[span(t, 4)], load_sem.at[0]),
        pltpu.make_async_copy(adj_h, adj, load_sem.at[1]),
        pltpu.make_async_copy(fields_h, fields, load_sem.at[2]),
        pltpu.make_async_copy(cls_h, cls, load_sem.at[3]),
        pltpu.make_async_copy(nbr_h, nbr, load_sem.at[4]),
        pltpu.make_async_copy(couple_h.at[:, :, lanes], slab, load_sem.at[5]),
        pltpu.make_async_copy(couple_h.at[:, own, :], rows_w, load_sem.at[6]),
    ]
    for load in loads:
        load.start()

    barrier = pltpu.get_barrier_semaphore()
    near_tiles, near_coef = (1, 15, 2, 4, 6, 8, 10, 12, 14), ((1, 0), (2, 0), (3, 0), (0, 1), (0, 3))
    for step in near_tiles:
        pl.semaphore_signal(barrier, inc=1, device_id=(tile_at(step), c), device_id_type=MESH)
    for dx, dz in near_coef:
        pl.semaphore_signal(barrier, inc=1, device_id=(t, peer(dx, dz)), device_id_type=MESH)
    for load in loads[:4]:
        load.wait()
    flat = t_all[span(t, 4)].reshape(4 * rows, 256)
    tt_src[...] = jnp.concatenate([flat, flat], axis=0).T
    af_all[own, :width] = adj[...]
    af_all[own, width:] = fields[...]
    pl.semaphore_wait(barrier, len(near_tiles) + len(near_coef))
    pl.semaphore_signal(z_known, inc=1, device_id=(t, peer(0, 1)), device_id_type=MESH)

    def remote(src, dst, send, recv, tile, coef):
        copy = pltpu.make_async_remote_copy(
            src_ref=src, dst_ref=dst, send_sem=send, recv_sem=recv,
            device_id=(tile, coef), device_id_type=MESH,
        )
        copy.start()
        return copy

    class Spread:
        def __init__(self, shard, first, send, recv, mate_send, mate_recv):
            self.shard, self.first = shard, first
            self.mate_send, self.mate_recv = mate_send, mate_recv
            mine = shard(t)
            self.copies = {
                s: remote(mine, mine, send.at[first + s], recv.at[first + s], tile_at(2 * s), c)
                for s in (4, 3, 5, 2, 6, 1, 7)
            }
            self.passed = [remote(mine, mine, mate_send.at[first], mate_recv.at[first], mate, c)]

        def pass_on(self):
            for s in (1, 7, 2, 6, 3, 5, 4):
                self.copies[s].wait_recv()
                came, slot = self.shard(tile_at(16 - 2 * s)), self.first + s
                self.passed.append(remote(came, came, self.mate_send.at[slot], self.mate_recv.at[slot], mate, c))

        def finish(self):
            for copy in self.passed:
                copy.wait_recv()

        def drain(self):
            for copy in list(self.copies.values()) + self.passed:
                copy.wait_send()

    class Gather:
        def __init__(self, buf, send, recv):
            self.copies = {}
            self.buf, self.send, self.recv = buf, send, recv

        def start(self, source, dx, dz, slot):
            block = self.buf.at[span(source, rows)]
            self.copies[slot] = remote(block, block, self.send.at[slot], self.recv.at[slot], t, peer(dx, dz))

        def along_z(self, *steps):
            for dz in steps:
                self.start(c, 0, dz, dz)

        def along_x(self):
            for dx in (2, 1, 3):
                self.start(c, dx, 0, 4 * dx)

        def begin(self):
            self.along_z(2, 1, 3)
            self.along_x()

        def relay(self, *steps):
            for dz in steps or (1, 3, 2):
                self.copies[dz].wait_recv()
                for dx in (2, 1, 3):
                    self.start(peer(0, 4 - dz), dx, 0, 4 * dx + dz)

        def finish(self):
            for dz in (0, 1, 3, 2):
                for dx in (1, 3, 2):
                    self.copies[4 * dx + dz].wait_recv()

        def drain(self):
            for copy in self.copies.values():
                copy.wait_send()

    gather = Gather(af_all, g_send, g_recv)
    gather_ends = Gather(ends_all, h_send, h_recv)
    gather_c = Gather(coup_all, c_send, c_recv)
    gather_s = Gather(s_all, s_send, s_recv)

    x_copies = [
        remote(tt_src.at[span(lax.rem(x + dx, 4), 64)], by_x.at[x], x_send.at[dx], x_recv.at[dx], t, peer(dx, 0))
        for dx in (2, 1, 3)
    ]
    edges = []
    for k, (src, dst) in enumerate(((adj, edge_a), (fields, edge_f), (cls, edge_c))):
        for side, (start, step) in enumerate(((0, 15), (width - LANE, 1))):
            slot = 2 * k + side
            edges.append(
                remote(src.at[:, pl.ds(start, LANE)], dst.at[side], e_send.at[slot], e_recv.at[slot], tile_at(step), c)
            )

    by_x[x] = tt_src[span(x, 64)]
    clsh[:, :width] = cls[...]
    gather.along_z(1, 3)
    gather.along_x()
    for copy in x_copies:
        copy.wait_recv()
    pl.semaphore_wait(z_known, 1)
    z_copies = {
        dz: remote(by_x.at[:, span(lax.rem(z + dz, 4), rows), :], by_z.at[z], z_send.at[dz], z_recv.at[dz], t, peer(0, dz))
        for dz in (2, 1, 3)
    }
    gather.along_z(2)
    by_z[z] = by_x[:, span(z, rows), :]
    low = lax.broadcasted_iota(jnp.int32, (rows, LANE), 1) < LANE // 2
    t_cols = {}

    def spread_quarter(dz):
        if dz:
            z_copies[dz].wait_recv()
        source_z = lax.rem(z + 4 - dz, 4)
        for half in range(2):
            block = jnp.where(low, by_z[source_z, 2 * half], by_z[source_z, 2 * half + 1])
            tt_all[source_z, span(t, rows), half * LANE : (half + 1) * LANE] = block
        t_cols[dz] = Spread(
            lambda tile: tt_all.at[source_z, span(tile, rows)], 8 * dz, u_send, u_recv, um_send, um_recv
        )

    spread_quarter(0)

    for edge in edges:
        edge.wait_recv()
    low_row = lax.broadcasted_iota(jnp.int32, (1, LANE), 1) < LANE // 2
    ends_all[own, :LANE] = jnp.where(low, edge_a[0], edge_a[1])
    ends_all[own, LANE:] = jnp.where(low, edge_f[0], edge_f[1])
    clsh[:, width:] = jnp.where(low_row, edge_c[0], edge_c[1])
    gather_ends.begin()
    gather.relay(1, 3)

    loads[4].wait()
    mask[...] = (nbr[...] >= 0).astype(F32)
    loads[5].wait()
    loads[6].wait()
    pick = (
        lax.broadcasted_iota(jnp.int32, (rows, LANE), 1)
        == lax.broadcasted_iota(jnp.int32, (rows, LANE), 0) + lax.rem(c, 8) * rows
    ).astype(F32).astype(BF16)
    for m in range(SLOTS):
        cols_w[m] = dot(pick, slab[SLOTS - 1 - m], 1, 1).astype(BF16)

    spread_quarter(1)
    spread_quarter(3)
    spread_quarter(2)
    t_rows = Spread(lambda tile: t_all.at[span(tile, 4)], 0, t_send, t_recv, tm_send, tm_recv)
    gather.relay(2)
    gather_ends.relay()

    def coupling(weights, inner, ends):
        product = jnp.concatenate([dot(weights, inner), dot(weights, ends)], axis=1)
        total = jnp.zeros((rows, width), F32)
        for m in range(SLOTS):
            shift = m - HW + (1 if m >= HW else 0)
            rolled = pltpu.roll(product[m * rows : (m + 1) * rows], (-shift) % wide, 1)
            total += rolled[:, :width] * mask[m : m + 1, :]
        return total

    for dz in (0, 1, 3):
        t_cols[dz].pass_on()
    gather.finish()
    t_cols[2].pass_on()
    gather_ends.finish()
    own_rows = rows_w[...].reshape(SLOTS * rows, 256)
    coup_all[own, :] = coupling(own_rows, af_all[:, width:], ends_all[:, LANE:]).astype(BF16)
    gather_c.begin()
    within = jnp.broadcast_to(jnp.bitwise_and(clsh[...], 3), (rows, wide))
    for source_z in range(4):
        for source_x in range(4):
            source = 4 * source_x + source_z
            block = slice(source * rows, (source + 1) * rows)
            values = af_all[block, :width].astype(F32)
            for k in range(4):
                at = ((4 * source_z + source_x) * 4 + k) * rows
                expanded[at : at + rows, :width] = jnp.where(within[:, :width] == k, values, 0.0).astype(BF16)

    for source_z in range(4):
        for source_x in range(4):
            source = 4 * source_x + source_z
            block = slice(source * rows, (source + 1) * rows)
            values = ends_all[block, :LANE].astype(F32)
            for k in range(4):
                at = ((4 * source_z + source_x) * 4 + k) * rows
                expanded[at : at + rows, width:] = jnp.where(within[:, width:] == k, values, 0.0).astype(BF16)
    product = jnp.zeros((256, wide), F32)
    for dz in (0, 1, 3, 2):
        t_cols[dz].finish()
        quarter = lax.rem(z + 4 - dz, 4)
        product += dot(tt_all[quarter], expanded[span(quarter, 256)])
    group = jnp.broadcast_to(lax.shift_right_arithmetic(clsh[...], jnp.full((1, wide), 2, jnp.int32)), (rows, wide))
    scattered = jnp.zeros((rows, wide), F32)
    for k in range(16):
        scattered += jnp.where(group == k, product[k * rows : (k + 1) * rows], 0.0)
    s_all[own, :] = scattered.astype(BF16)
    gather_s.begin()
    gather_c.relay()
    gather_s.relay()

    t_rows.pass_on()
    t_rows.finish()
    gather_c.finish()
    cls_own = jnp.broadcast_to(cls[...], (rows, width))
    applied = jnp.zeros((rows, width), F32)
    for b in range(4):
        product = dot(t_all[16 * b : 16 * b + 16].reshape(16 * rows, 256), coup_all[...])
        for k in range(16):
            applied += jnp.where(cls_own == 16 * b + k, product[k * rows : (k + 1) * rows], 0.0)
    fwd_ref[...] = (fields[...].astype(F32) - applied).astype(BF16)

    gather_s.finish()
    returned = coupling(cols_w[...].reshape(SLOTS * rows, 256), s_all[:, :width], s_all[:, width:])
    adjo_ref[...] = (adj[...].astype(F32) - returned).astype(BF16)

    for copy in x_copies + list(z_copies.values()) + edges:
        copy.wait_send()
    for group_copies in (t_rows, *t_cols.values(), gather, gather_ends, gather_c, gather_s):
        group_copies.drain()


def hand_over(fwd_ref, adj_ref, fwd_out, adj_out, sem):
    copies = [
        pltpu.make_async_copy(fwd_ref, fwd_out, sem.at[0]),
        pltpu.make_async_copy(adj_ref, adj_out, sem.at[1]),
    ]
    for copy in copies:
        copy.start()
    for copy in copies:
        copy.wait()


def local(fields, adjoints, couple, tmatrices, neighbours, classes):
    rows, width = fields.shape
    wide = width + LANE
    kr = couple.shape[1]
    dma = pltpu.SemaphoreType.DMA
    anywhere = pl.BlockSpec(memory_space=pl.ANY)
    vmem = pl.BlockSpec(memory_space=pltpu.VMEM)
    outputs = (jax.ShapeDtypeStruct((rows, width), BF16),) * 2
    operands = (fields, adjoints, couple, tmatrices, neighbours.T, classes.reshape(1, width))
    results = pl.pallas_call(
        kernel,
        out_shape=outputs,
        in_specs=[anywhere] * 6,
        out_specs=(vmem, vmem),
        scratch_shapes=[
            pltpu.VMEM((rows, width), BF16),
            pltpu.VMEM((rows, width), BF16),
            pltpu.VMEM((SLOTS, width), jnp.int32),
            pltpu.VMEM((1, width), jnp.int32),
            pltpu.VMEM((SLOTS, rows, kr), BF16),
            pltpu.VMEM((SLOTS, kr, LANE), BF16),
            pltpu.VMEM((SLOTS, rows, kr), BF16),
            pltpu.VMEM((SLOTS, width), F32),
            pltpu.VMEM((64, rows, kr), BF16),
            pltpu.VMEM((kr, LANE), BF16),
            pltpu.VMEM((4, 64, LANE), BF16),
            pltpu.VMEM((4, 4, rows, LANE), BF16),
            pltpu.VMEM((4, kr, 256), BF16),
            pltpu.VMEM((2, rows, LANE), BF16),
            pltpu.VMEM((2, rows, LANE), BF16),
            pltpu.VMEM((2, 1, LANE), jnp.int32),
            pltpu.VMEM((kr, 2 * width), BF16),
            pltpu.VMEM((kr, 2 * LANE), BF16),
            pltpu.VMEM((1, wide), jnp.int32),
            pltpu.VMEM((1024, wide), BF16),
            pltpu.VMEM((kr, width), BF16),
            pltpu.VMEM((kr, wide), BF16),
            dma((7,)),
        ]
        + [dma((8,))] * 4
        + [dma((32,))] * 4
        + [dma((4,))] * 4
        + [dma((6,))] * 2
        + [dma((16,))] * 8
        + [pltpu.SemaphoreType.REGULAR],
        compiler_params=pltpu.CompilerParams(
            collective_id=0, has_side_effects=True, vmem_limit_bytes=40 * 1024 * 1024
        ),
    )(*[pltpu.with_memory_space_constraint(v, pltpu.HBM) for v in operands])
    return pl.pallas_call(
        hand_over,
        out_shape=outputs,
        in_specs=[vmem, vmem],
        out_specs=(anywhere, anywhere),
        scratch_shapes=[dma((2,))],
        compiler_params=pltpu.CompilerParams(vmem_limit_bytes=1024 * 1024),
    )(*results)


def solution(mesh):
    placed = (
        P("coef", "tiles"),
        P("coef", "tiles"),
        P(),
        P("tiles", "coef", None),
        P("tiles", None),
        P("tiles"),
    )
    return jax.shard_map(
        local,
        mesh=mesh,
        in_specs=placed,
        out_specs=(P("coef", "tiles"), P("coef", "tiles")),
        check_vma=False,
    )
```

```python
import jax
import jax.numpy as jnp
from jax import lax
from jax.experimental import pallas as pl
from jax.experimental.pallas import tpu as pltpu
from jax.sharding import PartitionSpec as P

SLOTS = 30
HW = 15
LANE = 128
MESH = pl.DeviceIdType.MESH
F32 = jnp.float32
BF16 = jnp.bfloat16


def dot(a, b, lhs=1, rhs=0):
    return lax.dot_general(a, b, (((lhs,), (rhs,)), ((), ())), preferred_element_type=F32)


def kernel(
    fields_h, adj_h, couple_h, tmat_h, nbr_h, cls_h, fwd_ref, adjo_ref,
    fields, adj, nbr, cls, rows_w, slab, cols_w, mask, t_all, tt_src, by_x, by_z, tt_all,
    edge_f, edge_a, edge_c, af_all, ends_all, clsh, expanded, coup_all, s_all,
    load_sem, t_send, t_recv, tm_send, tm_recv, u_send, u_recv, um_send, um_recv,
    x_send, x_recv, z_send, z_recv, e_send, e_recv,
    g_send, g_recv, h_send, h_recv, c_send, c_recv, s_send, s_recv, z_known,
):
    rows, width = fields.shape
    wide = clsh.shape[1]
    t, c = lax.axis_index("tiles"), lax.axis_index("coef")
    x, z = c // 4, lax.rem(c, 4)
    mate = t + 1 - 2 * lax.rem(t, 2)

    def tile_at(step):
        return lax.rem(t + step, 16)

    def peer(dx, dz):
        return lax.rem(x + dx, 4) * 4 + lax.rem(z + dz, 4)

    def span(index, size):
        return pl.ds(pl.multiple_of(index * size, size), size)

    own = span(c, rows)
    lanes = span(c // 8, LANE)

    loads = [
        pltpu.make_async_copy(tmat_h, t_all.at[span(t, 4)], load_sem.at[0]),
        pltpu.make_async_copy(adj_h, adj, load_sem.at[1]),
        pltpu.make_async_copy(fields_h, fields, load_sem.at[2]),
        pltpu.make_async_copy(cls_h, cls, load_sem.at[3]),
        pltpu.make_async_copy(nbr_h, nbr, load_sem.at[4]),
        pltpu.make_async_copy(couple_h.at[:, :, lanes], slab, load_sem.at[5]),
        pltpu.make_async_copy(couple_h.at[:, own, :], rows_w, load_sem.at[6]),
    ]
    for load in loads:
        load.start()

    barrier = pltpu.get_barrier_semaphore()
    near_tiles, near_coef = (1, 15, 2, 4, 6, 8, 10, 12, 14), ((1, 0), (2, 0), (3, 0), (0, 1), (0, 3))
    for step in near_tiles:
        pl.semaphore_signal(barrier, inc=1, device_id=(tile_at(step), c), device_id_type=MESH)
    for dx, dz in near_coef:
        pl.semaphore_signal(barrier, inc=1, device_id=(t, peer(dx, dz)), device_id_type=MESH)
    for load in loads[:4]:
        load.wait()
    flat = t_all[span(t, 4)].reshape(4 * rows, 256)
    tt_src[...] = jnp.concatenate([flat, flat], axis=0).T
    af_all[own, :width] = adj[...]
    af_all[own, width:] = fields[...]
    pl.semaphore_wait(barrier, len(near_tiles) + len(near_coef))
    pl.semaphore_signal(z_known, inc=1, device_id=(t, peer(0, 1)), device_id_type=MESH)

    def remote(src, dst, send, recv, tile, coef):
        copy = pltpu.make_async_remote_copy(
            src_ref=src, dst_ref=dst, send_sem=send, recv_sem=recv,
            device_id=(tile, coef), device_id_type=MESH,
        )
        copy.start()
        return copy

    class Spread:
        def __init__(self, shard, first, send, recv, mate_send, mate_recv):
            self.shard, self.first = shard, first
            self.mate_send, self.mate_recv = mate_send, mate_recv
            mine = shard(t)
            self.copies = {
                s: remote(mine, mine, send.at[first + s], recv.at[first + s], tile_at(2 * s), c)
                for s in (4, 3, 5, 2, 6, 1, 7)
            }
            self.passed = [remote(mine, mine, mate_send.at[first], mate_recv.at[first], mate, c)]

        def pass_on(self):
            for s in (1, 7, 2, 6, 3, 5, 4):
                self.copies[s].wait_recv()
                came, slot = self.shard(tile_at(16 - 2 * s)), self.first + s
                self.passed.append(remote(came, came, self.mate_send.at[slot], self.mate_recv.at[slot], mate, c))

        def finish(self):
            for copy in self.passed:
                copy.wait_recv()

        def drain(self):
            for copy in list(self.copies.values()) + self.passed:
                copy.wait_send()

    class Gather:
        def __init__(self, buf, send, recv):
            self.copies = {}
            self.buf, self.send, self.recv = buf, send, recv

        def start(self, source, dx, dz, slot):
            block = self.buf.at[span(source, rows)]
            self.copies[slot] = remote(block, block, self.send.at[slot], self.recv.at[slot], t, peer(dx, dz))

        def along_z(self, *steps):
            for dz in steps:
                self.start(c, 0, dz, dz)

        def along_x(self):
            for dx in (2, 1, 3):
                self.start(c, dx, 0, 4 * dx)

        def begin(self):
            self.along_z(2, 1, 3)
            self.along_x()

        def relay(self, *steps):
            for dz in steps or (1, 3, 2):
                self.copies[dz].wait_recv()
                for dx in (2, 1, 3):
                    self.start(peer(0, 4 - dz), dx, 0, 4 * dx + dz)

        def finish(self):
            for dz in (0, 1, 3, 2):
                for dx in (1, 3, 2):
                    self.copies[4 * dx + dz].wait_recv()

        def drain(self):
            for copy in self.copies.values():
                copy.wait_send()

    gather = Gather(af_all, g_send, g_recv)
    gather_ends = Gather(ends_all, h_send, h_recv)
    gather_c = Gather(coup_all, c_send, c_recv)
    gather_s = Gather(s_all, s_send, s_recv)

    x_copies = [
        remote(tt_src.at[span(lax.rem(x + dx, 4), 64)], by_x.at[x], x_send.at[dx], x_recv.at[dx], t, peer(dx, 0))
        for dx in (2, 1, 3)
    ]
    edges = []
    for k, (src, dst) in enumerate(((adj, edge_a), (fields, edge_f), (cls, edge_c))):
        for side, (start, step) in enumerate(((0, 15), (width - LANE, 1))):
            slot = 2 * k + side
            edges.append(
                remote(src.at[:, pl.ds(start, LANE)], dst.at[side], e_send.at[slot], e_recv.at[slot], tile_at(step), c)
            )

    by_x[x] = tt_src[span(x, 64)]
    clsh[:, :width] = cls[...]
    gather.along_z(1, 3)
    for copy in x_copies:
        copy.wait_recv()
    pl.semaphore_wait(z_known, 1)
    z_copies = {
        dz: remote(by_x.at[:, span(lax.rem(z + dz, 4), rows), :], by_z.at[z], z_send.at[dz], z_recv.at[dz], t, peer(0, dz))
        for dz in (2, 1, 3)
    }
    gather.along_z(2)
    gather.along_x()
    by_z[z] = by_x[:, span(z, rows), :]
    low = lax.broadcasted_iota(jnp.int32, (rows, LANE), 1) < LANE // 2
    t_cols = {}

    def spread_quarter(dz):
        if dz:
            z_copies[dz].wait_recv()
        source_z = lax.rem(z + 4 - dz, 4)
        for half in range(2):
            block = jnp.where(low, by_z[source_z, 2 * half], by_z[source_z, 2 * half + 1])
            tt_all[source_z, span(t, rows), half * LANE : (half + 1) * LANE] = block
        t_cols[dz] = Spread(
            lambda tile: tt_all.at[source_z, span(tile, rows)], 8 * dz, u_send, u_recv, um_send, um_recv
        )

    spread_quarter(0)

    for edge in edges:
        edge.wait_recv()
    low_row = lax.broadcasted_iota(jnp.int32, (1, LANE), 1) < LANE // 2
    ends_all[own, :LANE] = jnp.where(low, edge_a[0], edge_a[1])
    ends_all[own, LANE:] = jnp.where(low, edge_f[0], edge_f[1])
    clsh[:, width:] = jnp.where(low_row, edge_c[0], edge_c[1])
    gather_ends.begin()
    gather.relay(1, 3)

    loads[4].wait()
    mask[...] = (nbr[...] >= 0).astype(F32)
    loads[5].wait()
    loads[6].wait()
    pick = (
        lax.broadcasted_iota(jnp.int32, (rows, LANE), 1)
        == lax.broadcasted_iota(jnp.int32, (rows, LANE), 0) + lax.rem(c, 8) * rows
    ).astype(F32).astype(BF16)
    for m in range(SLOTS):
        cols_w[m] = dot(pick, slab[SLOTS - 1 - m], 1, 1).astype(BF16)

    spread_quarter(1)
    spread_quarter(3)
    spread_quarter(2)
    t_rows = Spread(lambda tile: t_all.at[span(tile, 4)], 0, t_send, t_recv, tm_send, tm_recv)
    gather.relay(2)
    gather_ends.relay()

    def coupling(weights, inner, ends):
        product = jnp.concatenate([dot(weights, inner), dot(weights, ends)], axis=1)
        total = jnp.zeros((rows, width), F32)
        for m in range(SLOTS):
            shift = m - HW + (1 if m >= HW else 0)
            rolled = pltpu.roll(product[m * rows : (m + 1) * rows], (-shift) % wide, 1)
            total += rolled[:, :width] * mask[m : m + 1, :]
        return total

    for dz in (0, 1, 3):
        t_cols[dz].pass_on()
    gather.finish()
    t_cols[2].pass_on()
    gather_ends.finish()
    own_rows = rows_w[...].reshape(SLOTS * rows, 256)
    coup_all[own, :] = coupling(own_rows, af_all[:, width:], ends_all[:, LANE:]).astype(BF16)
    gather_c.begin()
    within = jnp.broadcast_to(jnp.bitwise_and(clsh[...], 3), (rows, wide))
    for source_z in range(4):
        for source_x in range(4):
            source = 4 * source_x + source_z
            block = slice(source * rows, (source + 1) * rows)
            values = af_all[block, :width].astype(F32)
            for k in range(4):
                at = ((4 * source_z + source_x) * 4 + k) * rows
                expanded[at : at + rows, :width] = jnp.where(within[:, :width] == k, values, 0.0).astype(BF16)

    for source_z in range(4):
        for source_x in range(4):
            source = 4 * source_x + source_z
            block = slice(source * rows, (source + 1) * rows)
            values = ends_all[block, :LANE].astype(F32)
            for k in range(4):
                at = ((4 * source_z + source_x) * 4 + k) * rows
                expanded[at : at + rows, width:] = jnp.where(within[:, width:] == k, values, 0.0).astype(BF16)
    product = jnp.zeros((256, wide), F32)
    for dz in (0, 1, 3, 2):
        t_cols[dz].finish()
        quarter = lax.rem(z + 4 - dz, 4)
        product += dot(tt_all[quarter], expanded[span(quarter, 256)])
    group = jnp.broadcast_to(lax.shift_right_arithmetic(clsh[...], jnp.full((1, wide), 2, jnp.int32)), (rows, wide))
    scattered = jnp.zeros((rows, wide), F32)
    for k in range(16):
        scattered += jnp.where(group == k, product[k * rows : (k + 1) * rows], 0.0)
    s_all[own, :] = scattered.astype(BF16)
    gather_s.begin()
    gather_c.relay()
    gather_s.relay()

    t_rows.pass_on()
    t_rows.finish()
    gather_c.finish()
    cls_own = jnp.broadcast_to(cls[...], (rows, width))
    applied = jnp.zeros((rows, width), F32)
    for b in range(4):
        product = dot(t_all[16 * b : 16 * b + 16].reshape(16 * rows, 256), coup_all[...])
        for k in range(16):
            applied += jnp.where(cls_own == 16 * b + k, product[k * rows : (k + 1) * rows], 0.0)
    fwd_ref[...] = (fields[...].astype(F32) - applied).astype(BF16)

    gather_s.finish()
    returned = coupling(cols_w[...].reshape(SLOTS * rows, 256), s_all[:, :width], s_all[:, width:])
    adjo_ref[...] = (adj[...].astype(F32) - returned).astype(BF16)

    for copy in x_copies + list(z_copies.values()) + edges:
        copy.wait_send()
    for group_copies in (t_rows, *t_cols.values(), gather, gather_ends, gather_c, gather_s):
        group_copies.drain()


def hand_over(fwd_ref, adj_ref, fwd_out, adj_out, sem):
    copies = [
        pltpu.make_async_copy(fwd_ref, fwd_out, sem.at[0]),
        pltpu.make_async_copy(adj_ref, adj_out, sem.at[1]),
    ]
    for copy in copies:
        copy.start()
    for copy in copies:
        copy.wait()


def local(fields, adjoints, couple, tmatrices, neighbours, classes):
    rows, width = fields.shape
    wide = width + LANE
    kr = couple.shape[1]
    dma = pltpu.SemaphoreType.DMA
    anywhere = pl.BlockSpec(memory_space=pl.ANY)
    vmem = pl.BlockSpec(memory_space=pltpu.VMEM)
    outputs = (jax.ShapeDtypeStruct((rows, width), BF16),) * 2
    operands = (fields, adjoints, couple, tmatrices, neighbours.T, classes.reshape(1, width))
    results = pl.pallas_call(
        kernel,
        out_shape=outputs,
        in_specs=[anywhere] * 6,
        out_specs=(vmem, vmem),
        scratch_shapes=[
            pltpu.VMEM((rows, width), BF16),
            pltpu.VMEM((rows, width), BF16),
            pltpu.VMEM((SLOTS, width), jnp.int32),
            pltpu.VMEM((1, width), jnp.int32),
            pltpu.VMEM((SLOTS, rows, kr), BF16),
            pltpu.VMEM((SLOTS, kr, LANE), BF16),
            pltpu.VMEM((SLOTS, rows, kr), BF16),
            pltpu.VMEM((SLOTS, width), F32),
            pltpu.VMEM((64, rows, kr), BF16),
            pltpu.VMEM((kr, LANE), BF16),
            pltpu.VMEM((4, 64, LANE), BF16),
            pltpu.VMEM((4, 4, rows, LANE), BF16),
            pltpu.VMEM((4, kr, 256), BF16),
            pltpu.VMEM((2, rows, LANE), BF16),
            pltpu.VMEM((2, rows, LANE), BF16),
            pltpu.VMEM((2, 1, LANE), jnp.int32),
            pltpu.VMEM((kr, 2 * width), BF16),
            pltpu.VMEM((kr, 2 * LANE), BF16),
            pltpu.VMEM((1, wide), jnp.int32),
            pltpu.VMEM((1024, wide), BF16),
            pltpu.VMEM((kr, width), BF16),
            pltpu.VMEM((kr, wide), BF16),
            dma((7,)),
        ]
        + [dma((8,))] * 4
        + [dma((32,))] * 4
        + [dma((4,))] * 4
        + [dma((6,))] * 2
        + [dma((16,))] * 8
        + [pltpu.SemaphoreType.REGULAR],
        compiler_params=pltpu.CompilerParams(
            collective_id=0, has_side_effects=True, vmem_limit_bytes=40 * 1024 * 1024
        ),
    )(*[pltpu.with_memory_space_constraint(v, pltpu.HBM) for v in operands])
    return pl.pallas_call(
        hand_over,
        out_shape=outputs,
        in_specs=[vmem, vmem],
        out_specs=(anywhere, anywhere),
        scratch_shapes=[dma((2,))],
        compiler_params=pltpu.CompilerParams(vmem_limit_bytes=1024 * 1024),
    )(*results)


def solution(mesh):
    placed = (
        P("coef", "tiles"),
        P("coef", "tiles"),
        P(),
        P("tiles", "coef", None),
        P("tiles", None),
        P("tiles"),
    )
    return jax.shard_map(
        local,
        mesh=mesh,
        in_specs=placed,
        out_specs=(P("coef", "tiles"), P("coef", "tiles")),
        check_vma=False,
    )
```
